32 devices in a mesh: grp: 2 (over x), ref: 16 (over z, y, core).
Axes of the slice: x: 2, y: 2, z: 4, core: 2. Of those that a mesh axis runs over, the one named last changes fastest.
Arguments:
- particles: bfloat16 [256, 512], P(('grp', 'ref')), may hold values from -30 to 30
- samples: bfloat16 [65536, 512], P('ref'), may hold values from -6 to 6
Outputs:
- moved: float32 [256, 512], P(('grp', 'ref'))
The draws below stay inside these ranges and needn't reach their ends.
All inputs are finite; a program needn't handle non-finite values.
Results may differ from the reference program's by a relative error of at most 0.0035.
Values may be sent and summed in bfloat16 or wider, within the bound.
No kernel may reach another device: no remote copies, remote signals or barrier semaphores. Data moves between devices by JAX's collectives and lax.ppermute only.
A program may use at most 128 MiB of HBM per device.

```python
import jax
import jax.numpy as jnp
from jax import lax

D = 512
KERNEL_WIDTH = 16
PARTICLES = 256
REFS = 65536


def draw_particles(key, part):
    values = jnp.clip(jax.random.normal(key, (PARTICLES, D), jnp.float32), -6.0, 6.0)
    return values.astype(jnp.bfloat16)


def steps_of(key, shape, split, low, top_value):
    def one(position, blocks):
        heights = jax.random.uniform(jax.random.fold_in(jax.random.fold_in(key, 6), position), (blocks,), jnp.float32, low / len(split), top_value / len(split))
        return jnp.repeat(jnp.exp(heights), shape[position] // blocks).reshape((-1,) + (1,) * (len(shape) - position - 1))

    level = one(*split[0])
    for cut in split[1:]:
        level = level * one(*cut)
    return level


def normal_values(rng, shape, width, bound, shards=(), kind=jnp.bfloat16):
    gain = steps_of(rng, shape, shards, -0.22, 0.18) if shards else 1.0
    result = jax.random.normal(rng, shape, jnp.float32) * width * gain
    return jnp.minimum(jnp.maximum(result, -bound), bound).astype(kind)


def setup_inputs(seed: int = 0) -> dict:
    arg_keys = jax.random.split(jax.random.key(seed), 3)
    return {
        "particles": draw_particles(jax.random.fold_in(arg_keys[2], 71), 0),
        "samples": normal_values(arg_keys[1], (REFS, D), 1.0, 6.0, ((0, 16),)),
    }


def square_norms(values):
    wide = values.astype(jnp.float32)
    return jnp.sum(wide * wide, axis=1)


def reference(particles, samples):
    step_size = 8.0
    masked_score = -1.0e30
    block_rows = min(256, PARTICLES)
    blocks = PARTICLES // block_rows
    part_sq = square_norms(particles)
    ref_sq = square_norms(samples)
    all_ids = jnp.arange(PARTICLES, dtype=jnp.int32)

    def one_block(inputs):
        row_block, row_sq, row_ids = inputs
        cross_scores = (2.0 * jnp.dot(row_block, samples.T, preferred_element_type=jnp.float32) - row_sq[:, None] - ref_sq[None, :]) / (2.0 * KERNEL_WIDTH)
        cross_top = jnp.max(cross_scores, axis=1)
        cross_weights = jnp.exp(cross_scores - cross_top[:, None])
        cross_total = jnp.sum(cross_weights, axis=1)
        cross_mean = jnp.dot(cross_weights.astype(jnp.bfloat16), samples, preferred_element_type=jnp.float32) / cross_total[:, None]
        self_scores = (2.0 * jnp.dot(row_block, particles.T, preferred_element_type=jnp.float32) - row_sq[:, None] - part_sq[None, :]) / (2.0 * KERNEL_WIDTH)
        diag_mask = row_ids[:, None] == all_ids[None, :]
        self_scores = jnp.where(diag_mask, masked_score, self_scores)
        self_top = jnp.max(self_scores, axis=1)
        self_weights = jnp.where(diag_mask, 0.0, jnp.exp(self_scores - self_top[:, None]))
        self_total = jnp.sum(self_weights, axis=1)
        self_mean = jnp.dot(self_weights.astype(jnp.bfloat16), particles, preferred_element_type=jnp.float32) / self_total[:, None]
        return row_block.astype(jnp.float32) + step_size * (cross_mean - self_mean)

    moved = lax.map(one_block, (particles.reshape(blocks, block_rows, D), part_sq.reshape(blocks, block_rows), all_ids.reshape(blocks, block_rows)))
    return moved.reshape(PARTICLES, D)
```

```python
import functools

import jax
import jax.numpy as jnp
from jax import lax
from jax.experimental import pallas as pl
from jax.experimental.pallas import tpu as pltpu
from jax.sharding import PartitionSpec as P

KERNEL_WIDTH = 16
STEP_SIZE = 8.0
LANES = 128
NT = (((1,), (1,)), ((), ()))
VMEM = pl.BlockSpec(memory_space=pltpu.VMEM)
F32 = jnp.float32
BF16 = jnp.bfloat16
HALF = 1.0 / (2.0 * KERNEL_WIDTH)


def lane_square_norms(values):
    partial = None
    for start in range(0, values.shape[1], LANES):
        wide = values[:, start : start + LANES].astype(F32)
        partial = wide * wide if partial is None else partial + wide * wide
    high = partial.astype(BF16)
    rest = partial - high.astype(F32)
    mid = rest.astype(BF16)
    low = (rest - mid.astype(F32)).astype(BF16)
    ones = jnp.ones((8, LANES), BF16)

    def summed(part):
        return lax.dot_general(ones, part, NT, preferred_element_type=F32)

    return summed(low) + summed(mid) + summed(high)


def norm_kernel(first, samples_ref, out_ref):
    count = out_ref.shape[1]
    tile = min(512, count)
    for start in range(0, count, tile):
        block = samples_ref[pl.ds(first + start, tile), :]
        out_ref[:, pl.ds(start, tile)] = lane_square_norms(block) * HALF


def sample_norms(samples, first, count):
    return pl.pallas_call(
        functools.partial(norm_kernel, first),
        out_shape=jax.ShapeDtypeStruct((8, count), F32),
        in_specs=[VMEM],
        out_specs=VMEM,
        compiler_params=pltpu.CompilerParams(vmem_limit_bytes=16 << 20),
        cost_estimate=pl.CostEstimate(
            flops=2 * count * samples.shape[1],
            bytes_accessed=2 * count * samples.shape[1],
            transcendentals=0,
        ),
        name="sample_norms",
    )(samples)


def cross_kernel(pieces, norm_parts, *refs):
    piece_refs = refs[:pieces]
    samples_ref = refs[pieces]
    norm_refs = refs[pieces + 1 : pieces + 1 + norm_parts]
    keep_ref, send_ref, group_ref, score_ref = refs[pieces + 1 + norm_parts :]
    width = samples_ref.shape[1]
    count = samples_ref.shape[0]
    group = jnp.concatenate([ref[...] for ref in piece_refs], axis=0)
    rows = group.shape[0]
    group_ref[...] = group
    wide = group.astype(F32)
    group_sq = jnp.sum(wide * wide, axis=1, keepdims=True) * HALF
    scaled = group * BF16(2.0 * HALF)
    per_part = count // norm_parts
    tile = min(1024, per_part)
    peak = jnp.full((rows, LANES), -jnp.inf, F32)
    for start in range(0, count, tile):
        scores = lax.dot_general(
            scaled, samples_ref[pl.ds(start, tile), :], NT, preferred_element_type=F32
        )
        norm_ref = norm_refs[start // per_part]
        scores = scores - group_sq - norm_ref[0:1, pl.ds(start % per_part, tile)]
        score_ref[:, pl.ds(start, tile)] = scores
        for lane in range(0, tile, LANES):
            peak = jnp.maximum(peak, scores[:, lane : lane + LANES])
    top = jnp.max(peak, axis=1, keepdims=True)
    partial = jnp.zeros((rows, LANES), F32)
    total_sum = jnp.zeros((rows, width), F32)
    for start in range(0, count, tile):
        weights = jnp.exp(score_ref[:, pl.ds(start, tile)] - top)
        for lane in range(0, tile, LANES):
            partial = partial + weights[:, lane : lane + LANES]
        total_sum = total_sum + jnp.dot(
            weights.astype(BF16), samples_ref[pl.ds(start, tile), :], preferred_element_type=F32
        )
    total = jnp.sum(partial, axis=1, keepdims=True)
    lane_id = lax.broadcasted_iota(jnp.int32, (rows, LANES), 1)
    stats = jnp.where(lane_id < LANES // 2, top, total)
    half = rows // 2
    for ref, first in ((keep_ref, 0), (send_ref, half)):
        ref[:, 0:width] = total_sum[first : first + half]
        ref[:, width : width + LANES] = stats[first : first + half]


def cross_terms(pieces, samples, norms):
    rows = sum(piece.shape[0] for piece in pieces)
    count, width = samples.shape
    part = jax.ShapeDtypeStruct((rows // 2, width + LANES), F32)
    return pl.pallas_call(
        functools.partial(cross_kernel, len(pieces), len(norms)),
        out_shape=(part, part, jax.ShapeDtypeStruct((rows, width), pieces[0].dtype)),
        in_specs=[VMEM] * (len(pieces) + 1 + len(norms)),
        out_specs=(VMEM, VMEM, VMEM),
        scratch_shapes=[pltpu.VMEM((rows, count), F32)],
        compiler_params=pltpu.CompilerParams(vmem_limit_bytes=32 << 20),
        cost_estimate=pl.CostEstimate(
            flops=4 * rows * count * width,
            bytes_accessed=2 * count * width,
            transcendentals=rows * count,
        ),
        name="cross_terms",
    )(*pieces, samples, *norms)


def split_stats(stats):
    lane_id = lax.broadcasted_iota(jnp.int32, stats.shape, 1)
    left = lane_id < LANES // 2
    turned = pltpu.roll(stats, LANES // 2, 1)
    return jnp.where(left, stats, turned), jnp.where(left, turned, stats)


def combined(left, right, width):
    left_top, left_total = split_stats(left[:, width : width + LANES])
    right_top, right_total = split_stats(right[:, width : width + LANES])
    top = jnp.maximum(left_top, right_top)
    left_scale = jnp.exp(left_top - top)
    right_scale = jnp.exp(right_top - top)
    sums = [
        left[:, lane : lane + LANES] * left_scale + right[:, lane : lane + LANES] * right_scale
        for lane in range(0, width, LANES)
    ]
    return sums, top, left_total * left_scale + right_total * right_scale


def combine_kernel(left_ref, right_ref, keep_ref, send_ref):
    width = left_ref.shape[1] - LANES
    sums, top, total = combined(left_ref[...], right_ref[...], width)
    lane_id = lax.broadcasted_iota(jnp.int32, top.shape, 1)
    tiles = sums + [jnp.where(lane_id < LANES // 2, top, total)]
    half = keep_ref.shape[0]
    for index, tile in enumerate(tiles):
        keep_ref[:, pl.ds(index * LANES, LANES)] = tile[:half]
        send_ref[:, pl.ds(index * LANES, LANES)] = tile[half:]


def combine(left, right):
    part = jax.ShapeDtypeStruct((left.shape[0] // 2, left.shape[1]), left.dtype)
    return pl.pallas_call(
        combine_kernel,
        out_shape=(part, part),
        in_specs=[VMEM, VMEM],
        out_specs=(VMEM, VMEM),
        name="combine",
    )(left, right)


def self_kernel(own_ref, group_ref, *refs):
    other_refs, out_ref = refs[:-1], refs[-1]
    own = own_ref[...]
    wide = own.astype(F32)
    own_sq = jnp.sum(wide * wide, axis=1, keepdims=True) * HALF
    scaled = own * BF16(2.0 * HALF)
    scores = []
    for ref in (group_ref,) + other_refs:
        columns = ref[...]
        dots = lax.dot_general(scaled, columns, NT, preferred_element_type=F32)
        scores.append(dots - own_sq - lane_square_norms(columns)[0:1] * HALF)
    same = lax.broadcasted_iota(jnp.int32, scores[0].shape, 0) == lax.broadcasted_iota(
        jnp.int32, scores[0].shape, 1
    )
    scores[0] = jnp.where(same, -1e30, scores[0])
    top = functools.reduce(
        jnp.maximum, [jnp.max(score, axis=1, keepdims=True) for score in scores]
    )
    weights = [jnp.exp(score - top) for score in scores]
    weights[0] = jnp.where(same, 0.0, weights[0])
    total = sum(jnp.sum(weight, axis=1, keepdims=True) for weight in weights)
    sums = sum(
        jnp.dot(weight.astype(BF16), ref[...], preferred_element_type=F32)
        for weight, ref in zip(weights, (group_ref,) + other_refs)
    )
    out_ref[...] = sums / total


def self_means(own, group, others):
    return pl.pallas_call(
        self_kernel,
        out_shape=jax.ShapeDtypeStruct(own.shape, F32),
        in_specs=[VMEM] * (2 + len(others)),
        out_specs=VMEM,
        name="self_means",
    )(own, group, *others)


def final_kernel(own_ref, left_ref, right_ref, self_ref, out_ref):
    width = own_ref.shape[1]
    sums, _, total = combined(left_ref[...], right_ref[...], width)
    scale = 1.0 / total
    for index, tile in enumerate(sums):
        lanes = pl.ds(index * LANES, LANES)
        out_ref[:, lanes] = own_ref[:, lanes].astype(F32) + STEP_SIZE * (
            tile * scale - self_ref[:, lanes]
        )


def final(own, left, right, self_mean):
    return pl.pallas_call(
        final_kernel,
        out_shape=jax.ShapeDtypeStruct(own.shape, F32),
        in_specs=[VMEM] * 4,
        out_specs=VMEM,
        name="final",
    )(own, left, right, self_mean)


def swap(values, bit):
    size = lax.axis_size("ref")
    return lax.ppermute(values, "ref", [(i, i ^ bit) for i in range(size)])


def per_device(particles, samples):
    ref_size = lax.axis_size("ref")
    grp_size = lax.axis_size("grp")
    bits = [1 << k for k in range(ref_size.bit_length() - 1)]
    assert ref_size == 1 << len(bits) and len(bits) >= 2
    norm_parts = 4
    per_part = samples.shape[0] // norm_parts
    norms = [sample_norms(samples, k * per_part, per_part) for k in range(norm_parts)]
    block = particles
    for bit in reversed(bits[2:]):
        block = jnp.concatenate([block, swap(block, bit)], axis=0)
    pieces = [block, swap(block, bits[1]), swap(block, bits[0]), swap(block, bits[0] | bits[1])]
    keep, send, group = cross_terms(pieces, samples, norms)
    others = [
        lax.ppermute(group, "grp", [(i, (i + k) % grp_size) for i in range(grp_size)])
        for k in range(1, grp_size)
    ]
    self_mean = self_means(particles, group, others)
    for bit in bits[:-1]:
        keep, send = combine(keep, swap(send, bit))
    return final(particles, keep, swap(send, bits[-1]), self_mean)


def solution(mesh):
    in_specs = (P(("grp", "ref"), None), P("ref", None))
    out_specs = P(("grp", "ref"), None)
    return jax.shard_map(
        per_device, mesh=mesh, in_specs=in_specs, out_specs=out_specs, check_vma=False
    )
```

```python
import functools

import jax
import jax.numpy as jnp
from jax import lax
from jax.experimental import pallas as pl
from jax.experimental.pallas import tpu as pltpu
from jax.sharding import PartitionSpec as P


KERNEL_WIDTH = 16
STEP_SIZE = 8.0
LANES = 128
NT = (((1,), (1,)), ((), ()))
VMEM = pl.BlockSpec(memory_space=pltpu.VMEM)
ANY = pl.BlockSpec(memory_space=pl.ANY)
HBM = pl.BlockSpec(memory_space=pltpu.HBM)
SMALL = 2 << 20
F32 = jnp.float32
BF16 = jnp.bfloat16
HALF = 1.0 / (2.0 * KERNEL_WIDTH)


def lane_square_norms(values):
    partial = None
    for start in range(0, values.shape[1], LANES):
        wide = values[:, start : start + LANES].astype(F32)
        partial = wide * wide if partial is None else partial + wide * wide
    high = partial.astype(BF16)
    rest = partial - high.astype(F32)
    mid = rest.astype(BF16)
    low = (rest - mid.astype(F32)).astype(BF16)
    ones = jnp.ones((8, LANES), BF16)

    def summed(part):
        return lax.dot_general(ones, part, NT, preferred_element_type=F32)

    return summed(low) + summed(mid) + summed(high)


def turned_block(block, turned_ref, norm_ref, columns):
    turned = jnp.transpose(block)
    turned_ref[:, columns] = turned
    wide = turned.astype(F32)
    norm = jnp.sum(wide * wide, axis=0, keepdims=True) * HALF
    norm_ref[:, columns] = jnp.broadcast_to(norm, (8, norm.shape[1]))


def prepare_kernel(first, samples_ref, *refs):
    turned_ref, norm_ref = refs[-2:]
    count = turned_ref.shape[1]
    tile = min(512, count)
    for start in range(0, count, tile):
        block = samples_ref[pl.ds(first + start, tile), :]
        turned_block(block, turned_ref, norm_ref, pl.ds(start, tile))


def prepare(samples, first, count, after=()):
    width = samples.shape[1]
    return pl.pallas_call(
        functools.partial(prepare_kernel, first),
        out_shape=(
            jax.ShapeDtypeStruct((width, count), samples.dtype),
            jax.ShapeDtypeStruct((8, count), F32),
        ),
        in_specs=[VMEM] + [ANY] * len(after),
        out_specs=(VMEM, VMEM),
        compiler_params=pltpu.CompilerParams(vmem_limit_bytes=SMALL),
        cost_estimate=pl.CostEstimate(
            flops=2 * count * width, bytes_accessed=4 * count * width, transcendentals=0
        ),
        name="prepare",
    )(samples, *after)


def stage_kernel(own_ref, samples_ref, own_out, samples_out, turned_out, norm_out, sems):
    count = samples_ref.shape[0]
    chunks = sems.shape[0] - 1
    size = count // chunks
    own_copy = pltpu.make_async_copy(own_ref, own_out, sems.at[chunks])
    own_copy.start()
    copies = []
    for k in range(chunks):
        rows = pl.ds(k * size, size)
        copies.append(
            pltpu.make_async_copy(samples_ref.at[rows], samples_out.at[rows], sems.at[k])
        )
        copies[-1].start()
    own_copy.wait()
    for k in range(chunks):
        copies[k].wait()
        if k * size < norm_out.shape[1]:
            rows = pl.ds(k * size, size)
            turned_block(samples_out[rows, :], turned_out, norm_out, rows)


def in_hbm(array):
    return pltpu.with_memory_space_constraint(array, pltpu.HBM)


def stage(own, samples, first_count, chunks):
    return pl.pallas_call(
        stage_kernel,
        out_shape=(
            pltpu.VMEM(own.shape, own.dtype),
            pltpu.VMEM(samples.shape, samples.dtype),
            pltpu.VMEM((samples.shape[1], first_count), samples.dtype),
            pltpu.VMEM((8, first_count), F32),
        ),
        in_specs=[HBM, HBM],
        out_specs=(VMEM, VMEM, VMEM, VMEM),
        scratch_shapes=[pltpu.SemaphoreType.DMA((chunks + 1,))],
        compiler_params=pltpu.CompilerParams(vmem_limit_bytes=SMALL),
        name="stage",
    )(in_hbm(own), in_hbm(samples))


def join_kernel(first_ref, second_ref, *refs):
    refs[-1][...] = jnp.concatenate([first_ref[...], second_ref[...]], axis=0)


def join(first, second, after=()):
    rows, width = first.shape
    return pl.pallas_call(
        join_kernel,
        out_shape=jax.ShapeDtypeStruct((2 * rows, width), first.dtype),
        in_specs=[VMEM, VMEM] + [ANY] * len(after),
        out_specs=VMEM,
        compiler_params=pltpu.CompilerParams(vmem_limit_bytes=SMALL),
        name="join",
    )(first, second, *after)


def packed(ref, sums, top, total):
    width = sums.shape[1]
    lane_id = lax.broadcasted_iota(jnp.int32, (sums.shape[0], LANES), 1)
    ref[:, 0:width] = sums
    ref[:, width : width + LANES] = jnp.where(lane_id < LANES // 2, top, total)


def cross_kernel(near_ref, far_ref, samples_ref, *refs):
    near_out, far_out = refs[-2:]
    turned_refs, norm_refs = refs[0:-2:2], refs[1:-2:2]
    group = jnp.concatenate([near_ref[...], far_ref[...]], axis=0)
    rows, _ = group.shape
    wide = group.astype(F32)
    group_sq = jnp.sum(wide * wide, axis=1, keepdims=True) * HALF
    scaled = group * BF16(2.0 * HALF)
    tiles, start = [], 0
    for first, last in ((0, 1), (1, len(turned_refs))):
        chunks = []
        for turned_ref, norm_ref in zip(turned_refs[first:last], norm_refs[first:last]):
            dots = jnp.dot(scaled, turned_ref[...], preferred_element_type=F32)
            chunks.append(dots - norm_ref[0:1, :])
        scores = jnp.concatenate(chunks, axis=1)
        count = scores.shape[1]
        lanes = [slice(lane, lane + LANES) for lane in range(0, count, LANES)]
        peak = functools.reduce(jnp.maximum, [scores[:, lane] for lane in lanes])
        top = jnp.max(peak, axis=1, keepdims=True)
        weights = jnp.exp(scores - top)
        partial = functools.reduce(jnp.add, [weights[:, lane] for lane in lanes])
        sums = jnp.dot(
            weights.astype(BF16), samples_ref[pl.ds(start, count), :], preferred_element_type=F32
        )
        tiles.append((top, partial, sums))
        start += count
    top = jnp.maximum(tiles[0][0], tiles[1][0])
    scales = [jnp.exp(tile[0] - top) for tile in tiles]
    partial = sum(tile[1] * scale for tile, scale in zip(tiles, scales))
    sums = sum(tile[2] * scale for tile, scale in zip(tiles, scales))
    total = jnp.sum(partial, axis=1, keepdims=True)
    top = top - group_sq
    half = rows // 2
    packed(near_out, sums[:half], top[:half], total[:half])
    packed(far_out, sums[half:], top[half:], total[half:])


def cross_terms(near, far, samples, prepared):
    count, width = samples.shape
    rows = near.shape[0] + far.shape[0]
    part = jax.ShapeDtypeStruct((rows // 2, width + LANES), F32)
    return pl.pallas_call(
        cross_kernel,
        out_shape=(part, part),
        in_specs=[VMEM] * (3 + 2 * len(prepared)),
        out_specs=(VMEM, VMEM),
        compiler_params=pltpu.CompilerParams(vmem_limit_bytes=12 << 20),
        cost_estimate=pl.CostEstimate(
            flops=4 * rows * count * width,
            bytes_accessed=4 * count * width,
            transcendentals=rows * count,
        ),
        name="cross_terms",
    )(near, far, samples, *[array for pair in prepared for array in pair])


def split_stats(stats):
    lane_id = lax.broadcasted_iota(jnp.int32, stats.shape, 1)
    left = lane_id < LANES // 2
    turned = pltpu.roll(stats, LANES // 2, 1)
    return jnp.where(left, stats, turned), jnp.where(left, turned, stats)


def three_parts(values):
    high = values.astype(BF16).astype(F32)
    rest = values - high
    mid = rest.astype(BF16).astype(F32)
    return high, mid, rest - mid


def parcel(ref, sums, top, total):
    lane_id = lax.broadcasted_iota(jnp.int32, top.shape, 1)
    stats = jnp.zeros_like(top)
    for index, part in enumerate(three_parts(top) + three_parts(total)):
        stats = jnp.where(lane_id == index, part, stats)
    for index, tile in enumerate(sums + [stats]):
        ref[:, pl.ds(index * LANES, LANES)] = tile.astype(BF16)


def opened(ref):
    tiles = [
        ref[:, pl.ds(lane, LANES)].astype(F32) for lane in range(0, ref.shape[1], LANES)
    ]
    stats = tiles.pop()
    parts = [jnp.broadcast_to(stats[:, k : k + 1], stats.shape) for k in range(6)]
    return tiles, parts[2] + parts[1] + parts[0], parts[5] + parts[4] + parts[3]


def loaded(ref):
    width = ref.shape[1] - LANES
    top, total = split_stats(ref[:, width : width + LANES])
    return [ref[:, pl.ds(lane, LANES)] for lane in range(0, width, LANES)], top, total


def combined(parts):
    tops = [part[1] for part in parts]
    top = functools.reduce(jnp.maximum, tops)
    scales = [jnp.exp(one - top) for one in tops]
    sums = [
        sum(tile * scale for tile, scale in zip(tiles, scales))
        for tiles in zip(*[part[0] for part in parts])
    ]
    return sums, top, sum(part[2] * scale for part, scale in zip(parts, scales))


def halves(sums, top, total, keep_ref, send_ref):
    half = keep_ref.shape[0]
    packed(
        keep_ref,
        jnp.concatenate([tile[:half] for tile in sums], axis=1),
        top[:half],
        total[:half],
    )
    parcel(send_ref, [tile[half:] for tile in sums], top[half:], total[half:])


def first_combine_kernel(left_ref, right_ref, centre_ref, keep_ref, send_ref):
    sums, top, total = combined([loaded(left_ref), loaded(right_ref)])
    sums = [
        tile - total * centre_ref[:, pl.ds(index * LANES, LANES)]
        for index, tile in enumerate(sums)
    ]
    halves(sums, top, total, keep_ref, send_ref)


def next_combine_kernel(left_ref, right_ref, keep_ref, send_ref):
    halves(*combined([loaded(left_ref), opened(right_ref)]), keep_ref, send_ref)


def combine(left, right, centres=None):
    rows, width = left.shape[0] // 2, left.shape[1]
    more = () if centres is None else (centres,)
    return pl.pallas_call(
        next_combine_kernel if centres is None else first_combine_kernel,
        out_shape=(
            jax.ShapeDtypeStruct((rows, width), F32),
            jax.ShapeDtypeStruct((rows, width), BF16),
        ),
        in_specs=[VMEM] * (2 + len(more)),
        out_specs=(VMEM, VMEM),
        compiler_params=pltpu.CompilerParams(vmem_limit_bytes=SMALL),
        name="combine",
    )(left, right, *more)


def self_kernel(near_ref, far_ref, *refs):
    visits = (len(refs) - 2) // 2
    visit_refs, centre_ref, out_refs = refs[:visits], refs[visits], refs[visits + 1 :]
    near = near_ref.shape[0]
    rows = jnp.concatenate([near_ref[...]] + [ref[...] for ref in visit_refs], axis=0)
    wide = rows.astype(F32)
    rows_sq = jnp.sum(wide * wide, axis=1, keepdims=True) * HALF
    scaled = rows * BF16(2.0 * HALF)
    columns = jnp.concatenate([near_ref[...], far_ref[...]], axis=0)
    dots = lax.dot_general(scaled, columns, NT, preferred_element_type=F32)
    scores = dots - rows_sq - lane_square_norms(columns)[0:1] * HALF
    row_id = lax.broadcasted_iota(jnp.int32, scores.shape, 0)
    same = (row_id == lax.broadcasted_iota(jnp.int32, scores.shape, 1)) & (row_id < near)
    scores = jnp.where(same, -1e30, scores)
    top = jnp.max(scores, axis=1, keepdims=True)
    weights = jnp.where(same, 0.0, jnp.exp(scores - top))
    total = jnp.sum(weights, axis=1, keepdims=True)
    sums = jnp.dot(weights.astype(BF16), columns, preferred_element_type=F32)
    centre_ref[...] = sums[:near] / total[:near]
    size = out_refs[0].shape[0]
    for first, ref in zip([0] + [near + k * size for k in range(visits)], out_refs):
        here = slice(first, first + size)
        packed(ref, sums[here], top[here], total[here])


def self_terms(near, far, visitors, size):
    width = near.shape[1]
    part = jax.ShapeDtypeStruct((size, width + LANES), F32)
    return pl.pallas_call(
        self_kernel,
        out_shape=(jax.ShapeDtypeStruct(near.shape, F32),) + (part,) * (1 + len(visitors)),
        in_specs=[VMEM] * (2 + len(visitors)),
        out_specs=(VMEM,) * (2 + len(visitors)),
        compiler_params=pltpu.CompilerParams(vmem_limit_bytes=SMALL),
        name="self_terms",
    )(near, far, *visitors)


def final_kernel(own_ref, left_ref, right_ref, centre_ref, *refs):
    self_refs, out_ref = refs[:-1], refs[-1]
    rows = own_ref.shape[0]
    sums, _, total = combined([loaded(left_ref), opened(right_ref)])
    self_sums, _, self_total = combined([loaded(ref) for ref in self_refs])
    scale = 1.0 / total
    self_scale = 1.0 / self_total
    for index, (tile, self_tile) in enumerate(zip(sums, self_sums)):
        lanes = pl.ds(index * LANES, LANES)
        cross_mean = tile * scale + centre_ref[0:rows, lanes]
        out_ref[:, lanes] = own_ref[:, lanes].astype(F32) + STEP_SIZE * (
            cross_mean - self_tile * self_scale
        )


def final(own, left, right, centres, self_parts):
    return pl.pallas_call(
        final_kernel,
        out_shape=jax.ShapeDtypeStruct(own.shape, F32),
        in_specs=[VMEM] * (4 + len(self_parts)),
        out_specs=VMEM,
        compiler_params=pltpu.CompilerParams(vmem_limit_bytes=SMALL),
        name="final",
    )(own, left, right, centres, *self_parts)


def swap(values, mask):
    size = lax.axis_size("ref")
    return lax.ppermute(values, "ref", [(i, i ^ mask) for i in range(size)])


def across(values, shift):
    groups, size = lax.axis_size("grp"), lax.axis_size("ref")
    pairs = [
        (g * size + i, (g + shift) % groups * size + (i ^ 1))
        for g in range(groups)
        for i in range(size)
    ]
    return lax.ppermute(values, ("grp", "ref"), pairs)


def swap_masks(size):
    count = size.bit_length() - 1
    assert size == 1 << count and count >= 3
    return [1] + [(1 << k) | 1 for k in range(1, count)]


def per_device(particles, samples):
    ref_size = lax.axis_size("ref")
    grp_size = lax.axis_size("grp")
    masks = swap_masks(ref_size)
    count = samples.shape[0]
    half = count // 2
    own, staged, *first_part = stage(particles, samples, half, 8)
    prepared = [first_part]
    block = own
    for mask in reversed(masks[1:]):
        other = swap(particles if block is own else block, mask)
        if block is not own and len(prepared) < 3:
            quarter = half // 2
            prepared.append(
                prepare(staged, half + (len(prepared) - 1) * quarter, quarter, [block])
            )
        block = join(block, other, prepared[-1][1:])
    far_block = swap(block, masks[0])
    keep, send = cross_terms(block, far_block, staged, prepared)
    visitors = [across(own, k) for k in range(1, grp_size)]
    centres, *self_parts = self_terms(block, far_block, visitors, own.shape[0])
    returned = [across(part, -k) for k, part in zip(range(1, grp_size), self_parts[1:])]
    keep, send = combine(keep, swap(send, masks[0]), centres)
    for mask in masks[1:-1]:
        keep, send = combine(keep, swap(send, mask))
    last = swap(send, masks[-1])
    return final(own, keep, last, centres, [self_parts[0]] + returned)


def solution(mesh):
    in_specs = (P(("grp", "ref"), None), P("ref", None))
    out_specs = P(("grp", "ref"), None)

    return jax.shard_map(
        per_device, mesh=mesh, in_specs=in_specs, out_specs=out_specs, check_vma=False
    )
```

```python
import functools

import jax
import jax.numpy as jnp
from jax import lax
from jax.experimental import pallas as pl
from jax.experimental.pallas import tpu as pltpu
from jax.sharding import PartitionSpec as P


KERNEL_WIDTH = 16
STEP_SIZE = 8.0
LANES = 128
NT = (((1,), (1,)), ((), ()))
VMEM = pl.BlockSpec(memory_space=pltpu.VMEM)
ANY = pl.BlockSpec(memory_space=pl.ANY)
HBM = pl.BlockSpec(memory_space=pltpu.HBM)
SMALL = 2 << 20
STAGED = 2
F32 = jnp.float32
BF16 = jnp.bfloat16
HALF = 1.0 / (2.0 * KERNEL_WIDTH)


def lane_square_norms(values):
    partial = None
    for start in range(0, values.shape[1], LANES):
        wide = values[:, start : start + LANES].astype(F32)
        partial = wide * wide if partial is None else partial + wide * wide
    high = partial.astype(BF16)
    rest = partial - high.astype(F32)
    mid = rest.astype(BF16)
    low = (rest - mid.astype(F32)).astype(BF16)
    ones = jnp.ones((8, LANES), BF16)

    def summed(part):
        return lax.dot_general(ones, part, NT, preferred_element_type=F32)

    return summed(low) + summed(mid) + summed(high)


def turned_block(block, turned_ref, norm_ref, columns):
    turned = jnp.transpose(block)
    turned_ref[:, columns] = turned
    wide = turned.astype(F32)
    norm = jnp.sum(wide * wide, axis=0, keepdims=True) * HALF
    norm_ref[:, columns] = jnp.broadcast_to(norm, (8, norm.shape[1]))


def prepare_kernel(first, samples_ref, *refs):
    turned_ref, norm_ref = refs[-2:]
    count = turned_ref.shape[1]
    tile = min(512, count)
    for start in range(0, count, tile):
        block = samples_ref[pl.ds(first + start, tile), :]
        turned_block(block, turned_ref, norm_ref, pl.ds(start, tile))


def prepare(samples, first, count, after=()):
    width = samples.shape[1]
    return pl.pallas_call(
        functools.partial(prepare_kernel, first),
        out_shape=(
            jax.ShapeDtypeStruct((width, count), samples.dtype),
            jax.ShapeDtypeStruct((8, count), F32),
        ),
        in_specs=[VMEM] + [ANY] * len(after),
        out_specs=(VMEM, VMEM),
        compiler_params=pltpu.CompilerParams(vmem_limit_bytes=SMALL),
        cost_estimate=pl.CostEstimate(
            flops=2 * count * width, bytes_accessed=4 * count * width, transcendentals=0
        ),
        name="prepare",
    )(samples, *after)


def stage_kernel(own_ref, samples_ref, own_out, samples_out, turned_out, norm_out, sems):
    count = samples_ref.shape[0]
    chunks = sems.shape[0] - 1
    size = count // chunks
    own_copy = pltpu.make_async_copy(own_ref, own_out, sems.at[chunks])
    own_copy.start()
    copies = []
    for k in range(chunks):
        rows = pl.ds(k * size, size)
        copies.append(
            pltpu.make_async_copy(samples_ref.at[rows], samples_out.at[rows], sems.at[k])
        )
        copies[-1].start()
    own_copy.wait()
    for k in range(chunks):
        copies[k].wait()
        if k * size < norm_out.shape[1]:
            rows = pl.ds(k * size, size)
            turned_block(samples_out[rows, :], turned_out, norm_out, rows)


def in_hbm(array):
    return pltpu.with_memory_space_constraint(array, pltpu.HBM)


def stage(own, samples, first_count, chunks):
    return pl.pallas_call(
        stage_kernel,
        out_shape=(
            pltpu.VMEM(own.shape, own.dtype),
            pltpu.VMEM(samples.shape, samples.dtype),
            pltpu.VMEM((samples.shape[1], first_count), samples.dtype),
            pltpu.VMEM((8, first_count), F32),
        ),
        in_specs=[HBM, HBM],
        out_specs=(VMEM, VMEM, VMEM, VMEM),
        scratch_shapes=[pltpu.SemaphoreType.DMA((chunks + 1,))],
        compiler_params=pltpu.CompilerParams(vmem_limit_bytes=SMALL),
        name="stage",
    )(in_hbm(own), in_hbm(samples))


def join_kernel(count, *refs):
    refs[-1][...] = jnp.concatenate([ref[...] for ref in refs[:count]], axis=0)


def join(blocks, after=()):
    rows, width = blocks[0].shape
    return pl.pallas_call(
        functools.partial(join_kernel, len(blocks)),
        out_shape=jax.ShapeDtypeStruct((len(blocks) * rows, width), blocks[0].dtype),
        in_specs=[VMEM] * len(blocks) + [ANY] * len(after),
        out_specs=VMEM,
        compiler_params=pltpu.CompilerParams(vmem_limit_bytes=SMALL),
        name="join",
    )(*blocks, *after)


def packed(ref, sums, top, total):
    width = sums.shape[1]
    lane_id = lax.broadcasted_iota(jnp.int32, (sums.shape[0], LANES), 1)
    ref[:, 0:width] = sums
    ref[:, width : width + LANES] = jnp.where(lane_id < LANES // 2, top, total)


def cross_kernel(near_ref, far_ref, samples_ref, *refs):
    near_out, far_out = refs[-2:]
    turned_refs, norm_refs = refs[0:-2:2], refs[1:-2:2]
    group = jnp.concatenate([near_ref[...], far_ref[...]], axis=0)
    rows, _ = group.shape
    wide = group.astype(F32)
    group_sq = jnp.sum(wide * wide, axis=1, keepdims=True) * HALF
    scaled = group * BF16(2.0 * HALF)
    tiles, start = [], 0
    for first, last in ((0, 1), (1, len(turned_refs))):
        chunks = []
        for turned_ref, norm_ref in zip(turned_refs[first:last], norm_refs[first:last]):
            dots = jnp.dot(scaled, turned_ref[...], preferred_element_type=F32)
            chunks.append(dots - norm_ref[0:1, :])
        scores = jnp.concatenate(chunks, axis=1)
        count = scores.shape[1]
        lanes = [slice(lane, lane + LANES) for lane in range(0, count, LANES)]
        peak = functools.reduce(jnp.maximum, [scores[:, lane] for lane in lanes])
        top = jnp.max(peak, axis=1, keepdims=True)
        weights = jnp.exp(scores - top)
        partial = functools.reduce(jnp.add, [weights[:, lane] for lane in lanes])
        sums = jnp.dot(
            weights.astype(BF16), samples_ref[pl.ds(start, count), :], preferred_element_type=F32
        )
        tiles.append((top, partial, sums))
        start += count
    top = jnp.maximum(tiles[0][0], tiles[1][0])
    scales = [jnp.exp(tile[0] - top) for tile in tiles]
    partial = sum(tile[1] * scale for tile, scale in zip(tiles, scales))
    sums = sum(tile[2] * scale for tile, scale in zip(tiles, scales))
    total = jnp.sum(partial, axis=1, keepdims=True)
    top = top - group_sq
    half = rows // 2
    packed(near_out, sums[:half], top[:half], total[:half])
    packed(far_out, sums[half:], top[half:], total[half:])


def cross_terms(near, far, samples, prepared):
    count, width = samples.shape
    rows = near.shape[0] + far.shape[0]
    part = jax.ShapeDtypeStruct((rows // 2, width + LANES), F32)
    return pl.pallas_call(
        cross_kernel,
        out_shape=(part, part),
        in_specs=[VMEM] * (3 + 2 * len(prepared)),
        out_specs=(VMEM, VMEM),
        compiler_params=pltpu.CompilerParams(vmem_limit_bytes=12 << 20),
        cost_estimate=pl.CostEstimate(
            flops=4 * rows * count * width,
            bytes_accessed=4 * count * width,
            transcendentals=rows * count,
        ),
        name="cross_terms",
    )(near, far, samples, *[array for pair in prepared for array in pair])


def split_stats(stats):
    lane_id = lax.broadcasted_iota(jnp.int32, stats.shape, 1)
    left = lane_id < LANES // 2
    turned = pltpu.roll(stats, LANES // 2, 1)
    return jnp.where(left, stats, turned), jnp.where(left, turned, stats)


def three_parts(values):
    high = values.astype(BF16).astype(F32)
    rest = values - high
    mid = rest.astype(BF16).astype(F32)
    return high, mid, rest - mid


def parcel(ref, sums, top, total):
    lane_id = lax.broadcasted_iota(jnp.int32, top.shape, 1)
    stats = jnp.zeros_like(top)
    for index, part in enumerate(three_parts(top) + three_parts(total)):
        stats = jnp.where(lane_id == index, part, stats)
    for index, tile in enumerate(sums + [stats]):
        ref[:, pl.ds(index * LANES, LANES)] = tile.astype(BF16)


def opened(ref):
    tiles = [
        ref[:, pl.ds(lane, LANES)].astype(F32) for lane in range(0, ref.shape[1], LANES)
    ]
    stats = tiles.pop()
    parts = [jnp.broadcast_to(stats[:, k : k + 1], stats.shape) for k in range(6)]
    return tiles, parts[2] + parts[1] + parts[0], parts[5] + parts[4] + parts[3]


def loaded(ref):
    width = ref.shape[1] - LANES
    top, total = split_stats(ref[:, width : width + LANES])
    return [ref[:, pl.ds(lane, LANES)] for lane in range(0, width, LANES)], top, total


def combined(parts):
    tops = [part[1] for part in parts]
    top = functools.reduce(jnp.maximum, tops)
    scales = [jnp.exp(one - top) for one in tops]
    sums = [
        sum(tile * scale for tile, scale in zip(tiles, scales))
        for tiles in zip(*[part[0] for part in parts])
    ]
    return sums, top, sum(part[2] * scale for part, scale in zip(parts, scales))


def shared_out(sums, top, total, keep_ref, send_refs):
    rows = keep_ref.shape[0]
    packed(
        keep_ref,
        jnp.concatenate([tile[:rows] for tile in sums], axis=1),
        top[:rows],
        total[:rows],
    )
    for index, ref in enumerate(send_refs):
        here = slice((index + 1) * rows, (index + 2) * rows)
        parcel(ref, [tile[here] for tile in sums], top[here], total[here])


def first_combine_kernel(left_ref, right_ref, centre_ref, keep_ref, *send_refs):
    sums, top, total = combined([loaded(left_ref), loaded(right_ref)])
    sums = [
        tile - total * centre_ref[:, pl.ds(index * LANES, LANES)]
        for index, tile in enumerate(sums)
    ]
    shared_out(sums, top, total, keep_ref, send_refs)


def next_combine_kernel(left_ref, right_ref, keep_ref, *send_refs):
    shared_out(*combined([loaded(left_ref), opened(right_ref)]), keep_ref, send_refs)


def combine(left, right, sends, centres=None):
    rows, width = left.shape[0] // (1 + sends), left.shape[1]
    more = () if centres is None else (centres,)
    return pl.pallas_call(
        next_combine_kernel if centres is None else first_combine_kernel,
        out_shape=(jax.ShapeDtypeStruct((rows, width), F32),)
        + (jax.ShapeDtypeStruct((rows, width), BF16),) * sends,
        in_specs=[VMEM] * (2 + len(more)),
        out_specs=(VMEM,) * (1 + sends),
        compiler_params=pltpu.CompilerParams(vmem_limit_bytes=SMALL),
        name="combine",
    )(left, right, *more)


def self_kernel(near_ref, far_ref, *refs):
    visits = (len(refs) - 2) // 2
    visit_refs, centre_ref, out_refs = refs[:visits], refs[visits], refs[visits + 1 :]
    near = near_ref.shape[0]
    rows = jnp.concatenate([near_ref[...]] + [ref[...] for ref in visit_refs], axis=0)
    wide = rows.astype(F32)
    rows_sq = jnp.sum(wide * wide, axis=1, keepdims=True) * HALF
    scaled = rows * BF16(2.0 * HALF)
    columns = jnp.concatenate([near_ref[...], far_ref[...]], axis=0)
    dots = lax.dot_general(scaled, columns, NT, preferred_element_type=F32)
    scores = dots - rows_sq - lane_square_norms(columns)[0:1] * HALF
    row_id = lax.broadcasted_iota(jnp.int32, scores.shape, 0)
    same = (row_id == lax.broadcasted_iota(jnp.int32, scores.shape, 1)) & (row_id < near)
    scores = jnp.where(same, -1e30, scores)
    top = jnp.max(scores, axis=1, keepdims=True)
    weights = jnp.where(same, 0.0, jnp.exp(scores - top))
    total = jnp.sum(weights, axis=1, keepdims=True)
    sums = jnp.dot(weights.astype(BF16), columns, preferred_element_type=F32)
    centre_ref[...] = sums[:near] / total[:near]
    size = out_refs[0].shape[0]
    for first, ref in zip([0] + [near + k * size for k in range(visits)], out_refs):
        here = slice(first, first + size)
        packed(ref, sums[here], top[here], total[here])


def self_terms(near, far, visitors, size):
    width = near.shape[1]
    part = jax.ShapeDtypeStruct((size, width + LANES), F32)
    return pl.pallas_call(
        self_kernel,
        out_shape=(jax.ShapeDtypeStruct(near.shape, F32),) + (part,) * (1 + len(visitors)),
        in_specs=[VMEM] * (2 + len(visitors)),
        out_specs=(VMEM,) * (2 + len(visitors)),
        compiler_params=pltpu.CompilerParams(vmem_limit_bytes=SMALL),
        name="self_terms",
    )(near, far, *visitors)


def final_kernel(arrived, own_ref, left_ref, centre_ref, *refs):
    right_refs, self_refs, out_ref = refs[:arrived], refs[arrived:-1], refs[-1]
    rows = own_ref.shape[0]
    sums, _, total = combined([loaded(left_ref)] + [opened(ref) for ref in right_refs])
    self_sums, _, self_total = combined([loaded(ref) for ref in self_refs])
    scale = 1.0 / total
    self_scale = 1.0 / self_total
    for index, (tile, self_tile) in enumerate(zip(sums, self_sums)):
        lanes = pl.ds(index * LANES, LANES)
        cross_mean = tile * scale + centre_ref[0:rows, lanes]
        out_ref[:, lanes] = own_ref[:, lanes].astype(F32) + STEP_SIZE * (
            cross_mean - self_tile * self_scale
        )


def final(own, left, centres, rights, self_parts):
    return pl.pallas_call(
        functools.partial(final_kernel, len(rights)),
        out_shape=jax.ShapeDtypeStruct(own.shape, F32),
        in_specs=[VMEM] * (3 + len(rights) + len(self_parts)),
        out_specs=VMEM,
        compiler_params=pltpu.CompilerParams(vmem_limit_bytes=SMALL),
        name="final",
    )(own, left, centres, *rights, *self_parts)


def swap(values, mask):
    size = lax.axis_size("ref")
    return lax.ppermute(values, "ref", [(i, i ^ mask) for i in range(size)])


def across(values, shift):
    groups, size = lax.axis_size("grp"), lax.axis_size("ref")
    pairs = [
        (g * size + i, (g + shift) % groups * size + (i ^ 1))
        for g in range(groups)
        for i in range(size)
    ]
    return lax.ppermute(values, ("grp", "ref"), pairs)


def swap_masks(size):
    count = size.bit_length() - 1
    assert size == 1 << count and count >= 4
    low, high = 1 << (count - 2), 1 << (count - 1)
    singles = [1] + [(1 << k) | 1 for k in range(1, count - 2)]
    return singles, [high | low | 1, low, high | 1]


def per_device(particles, samples):
    grp_size = lax.axis_size("grp")
    singles, triple = swap_masks(lax.axis_size("ref"))
    count = samples.shape[0]
    own, staged, *first_part = stage(particles, samples, count * STAGED // 4, 8)
    prepared = [first_part]
    others = [swap(particles, mask) for mask in triple]
    block = join([own] + others, first_part[1:])
    prepared += [
        prepare(staged, part * count // 4, count // 4, [block]) for part in range(STAGED, 4)
    ]
    for mask in reversed(singles[1:]):
        block = join([block, swap(block, mask)], prepared[-1][1:])
    far_block = swap(block, singles[0])
    keep, send = cross_terms(block, far_block, staged, prepared)
    visitors = [across(own, k) for k in range(1, grp_size)]
    centres, *self_parts = self_terms(block, far_block, visitors, own.shape[0])
    returned = [across(part, -k) for k, part in zip(range(1, grp_size), self_parts[1:])]
    sends, more = [send], (centres,)
    for index, mask in enumerate(singles):
        count = 1 if index < len(singles) - 1 else len(triple)
        keep, *sends = combine(keep, swap(sends[0], mask), count, *more)
        more = ()
    rights = [swap(part, mask) for part, mask in zip(sends, triple)]
    return final(own, keep, centres, rights, [self_parts[0]] + returned)


def solution(mesh):
    in_specs = (P(("grp", "ref"), None), P("ref", None))
    out_specs = P(("grp", "ref"), None)

    return jax.shard_map(
        per_device, mesh=mesh, in_specs=in_specs, out_specs=out_specs, check_vma=False
    )
```

```python
import functools

import jax
import jax.numpy as jnp
from jax import lax
from jax.experimental import pallas as pl
from jax.experimental.pallas import tpu as pltpu
from jax.sharding import PartitionSpec as P


KERNEL_WIDTH = 16
STEP_SIZE = 8.0
LANES = 128
NT = (((1,), (1,)), ((), ()))
VMEM = pl.BlockSpec(memory_space=pltpu.VMEM)
ANY = pl.BlockSpec(memory_space=pl.ANY)
HBM = pl.BlockSpec(memory_space=pltpu.HBM)
SMALL = 2 << 20
STAGED = 2
F32 = jnp.float32
BF16 = jnp.bfloat16
HALF = 1.0 / (2.0 * KERNEL_WIDTH)


def lane_square_norms(values):
    partial = None
    for start in range(0, values.shape[1], LANES):
        wide = values[:, start : start + LANES].astype(F32)
        partial = wide * wide if partial is None else partial + wide * wide
    high = partial.astype(BF16)
    rest = partial - high.astype(F32)
    mid = rest.astype(BF16)
    low = (rest - mid.astype(F32)).astype(BF16)
    ones = jnp.ones((8, LANES), BF16)

    def summed(part):
        return lax.dot_general(ones, part, NT, preferred_element_type=F32)

    return summed(low) + summed(mid) + summed(high)


def turned_block(block, turned_ref, norm_ref, columns):
    turned = jnp.transpose(block)
    turned_ref[:, columns] = turned
    wide = turned.astype(F32)
    norm = jnp.sum(wide * wide, axis=0, keepdims=True) * HALF
    norm_ref[:, columns] = jnp.broadcast_to(norm, (8, norm.shape[1]))


def prepare_kernel(first, samples_ref, *refs):
    turned_ref, norm_ref = refs[-2:]
    count = turned_ref.shape[1]
    tile = min(512, count)
    for start in range(0, count, tile):
        block = samples_ref[pl.ds(first + start, tile), :]
        turned_block(block, turned_ref, norm_ref, pl.ds(start, tile))


def prepare(samples, first, count, after=()):
    width = samples.shape[1]
    return pl.pallas_call(
        functools.partial(prepare_kernel, first),
        out_shape=(
            jax.ShapeDtypeStruct((width, count), samples.dtype),
            jax.ShapeDtypeStruct((8, count), F32),
        ),
        in_specs=[VMEM] + [ANY] * len(after),
        out_specs=(VMEM, VMEM),
        compiler_params=pltpu.CompilerParams(vmem_limit_bytes=SMALL),
        cost_estimate=pl.CostEstimate(
            flops=2 * count * width, bytes_accessed=4 * count * width, transcendentals=0
        ),
        name="prepare",
    )(samples, *after)


def stage_kernel(own_ref, samples_ref, own_out, samples_out, turned_out, norm_out, sems):
    count = samples_ref.shape[0]
    chunks = sems.shape[0] - 1
    size = count // chunks
    own_copy = pltpu.make_async_copy(own_ref, own_out, sems.at[chunks])
    own_copy.start()
    copies = []
    for k in range(chunks):
        rows = pl.ds(k * size, size)
        copies.append(
            pltpu.make_async_copy(samples_ref.at[rows], samples_out.at[rows], sems.at[k])
        )
        copies[-1].start()
    own_copy.wait()
    for k in range(chunks):
        copies[k].wait()
        if k * size < norm_out.shape[1]:
            rows = pl.ds(k * size, size)
            turned_block(samples_out[rows, :], turned_out, norm_out, rows)


def in_hbm(array):
    return pltpu.with_memory_space_constraint(array, pltpu.HBM)


def stage(own, samples, first_count, chunks):
    return pl.pallas_call(
        stage_kernel,
        out_shape=(
            pltpu.VMEM(own.shape, own.dtype),
            pltpu.VMEM(samples.shape, samples.dtype),
            pltpu.VMEM((samples.shape[1], first_count), samples.dtype),
            pltpu.VMEM((8, first_count), F32),
        ),
        in_specs=[HBM, HBM],
        out_specs=(VMEM, VMEM, VMEM, VMEM),
        scratch_shapes=[pltpu.SemaphoreType.DMA((chunks + 1,))],
        compiler_params=pltpu.CompilerParams(vmem_limit_bytes=SMALL),
        name="stage",
    )(in_hbm(own), in_hbm(samples))


def join_kernel(count, runs, *refs):
    blocks = [ref[...] for ref in refs[:count]]
    size = blocks[0].shape[0] // runs
    refs[-1][...] = jnp.concatenate(
        [block[run * size : (run + 1) * size] for run in range(runs) for block in blocks], axis=0
    )


def join(blocks, runs, after=()):
    rows, width = blocks[0].shape
    return pl.pallas_call(
        functools.partial(join_kernel, len(blocks), runs),
        out_shape=jax.ShapeDtypeStruct((len(blocks) * rows, width), blocks[0].dtype),
        in_specs=[VMEM] * len(blocks) + [ANY] * len(after),
        out_specs=VMEM,
        compiler_params=pltpu.CompilerParams(vmem_limit_bytes=SMALL),
        name="join",
    )(*blocks, *after)


def packed(ref, sums, top, total):
    width = sums.shape[1]
    lane_id = lax.broadcasted_iota(jnp.int32, (sums.shape[0], LANES), 1)
    ref[:, 0:width] = sums
    ref[:, width : width + LANES] = jnp.where(lane_id < LANES // 2, top, total)


def cross_kernel(near_ref, far_ref, samples_ref, *refs):
    near_out, far_out = refs[-2:]
    turned_refs, norm_refs = refs[0:-2:2], refs[1:-2:2]
    group = jnp.concatenate([near_ref[...], far_ref[...]], axis=0)
    rows, _ = group.shape
    wide = group.astype(F32)
    group_sq = jnp.sum(wide * wide, axis=1, keepdims=True) * HALF
    scaled = group * BF16(2.0 * HALF)
    tiles, start = [], 0
    for first, last in ((0, 1), (1, len(turned_refs))):
        chunks = []
        for turned_ref, norm_ref in zip(turned_refs[first:last], norm_refs[first:last]):
            dots = jnp.dot(scaled, turned_ref[...], preferred_element_type=F32)
            chunks.append(dots - norm_ref[0:1, :])
        scores = jnp.concatenate(chunks, axis=1)
        count = scores.shape[1]
        lanes = [slice(lane, lane + LANES) for lane in range(0, count, LANES)]
        peak = functools.reduce(jnp.maximum, [scores[:, lane] for lane in lanes])
        top = jnp.max(peak, axis=1, keepdims=True)
        weights = jnp.exp(scores - top)
        partial = functools.reduce(jnp.add, [weights[:, lane] for lane in lanes])
        sums = jnp.dot(
            weights.astype(BF16), samples_ref[pl.ds(start, count), :], preferred_element_type=F32
        )
        tiles.append((top, partial, sums))
        start += count
    top = jnp.maximum(tiles[0][0], tiles[1][0])
    scales = [jnp.exp(tile[0] - top) for tile in tiles]
    partial = sum(tile[1] * scale for tile, scale in zip(tiles, scales))
    sums = sum(tile[2] * scale for tile, scale in zip(tiles, scales))
    total = jnp.sum(partial, axis=1, keepdims=True)
    top = top - group_sq
    half = rows // 2
    packed(near_out, sums[:half], top[:half], total[:half])
    packed(far_out, sums[half:], top[half:], total[half:])


def cross_terms(near, far, samples, prepared):
    count, width = samples.shape
    rows = near.shape[0] + far.shape[0]
    part = jax.ShapeDtypeStruct((rows // 2, width + LANES), F32)
    return pl.pallas_call(
        cross_kernel,
        out_shape=(part, part),
        in_specs=[VMEM] * (3 + 2 * len(prepared)),
        out_specs=(VMEM, VMEM),
        compiler_params=pltpu.CompilerParams(vmem_limit_bytes=12 << 20),
        cost_estimate=pl.CostEstimate(
            flops=4 * rows * count * width,
            bytes_accessed=4 * count * width,
            transcendentals=rows * count,
        ),
        name="cross_terms",
    )(near, far, samples, *[array for pair in prepared for array in pair])


def split_stats(stats):
    lane_id = lax.broadcasted_iota(jnp.int32, stats.shape, 1)
    left = lane_id < LANES // 2
    turned = pltpu.roll(stats, LANES // 2, 1)
    return jnp.where(left, stats, turned), jnp.where(left, turned, stats)


def three_parts(values):
    high = values.astype(BF16).astype(F32)
    rest = values - high
    mid = rest.astype(BF16).astype(F32)
    return high, mid, rest - mid


def parcel(ref, sums, top, total):
    lane_id = lax.broadcasted_iota(jnp.int32, top.shape, 1)
    stats = jnp.zeros_like(top)
    for index, part in enumerate(three_parts(top) + three_parts(total)):
        stats = jnp.where(lane_id == index, part, stats)
    for index, tile in enumerate(sums + [stats]):
        ref[:, pl.ds(index * LANES, LANES)] = tile.astype(BF16)


def opened(ref):
    tiles = [
        ref[:, pl.ds(lane, LANES)].astype(F32) for lane in range(0, ref.shape[1], LANES)
    ]
    stats = tiles.pop()
    parts = [jnp.broadcast_to(stats[:, k : k + 1], stats.shape) for k in range(6)]
    return tiles, parts[2] + parts[1] + parts[0], parts[5] + parts[4] + parts[3]


def loaded(ref):
    width = ref.shape[1] - LANES
    top, total = split_stats(ref[:, width : width + LANES])
    return [ref[:, pl.ds(lane, LANES)] for lane in range(0, width, LANES)], top, total


def combined(parts):
    tops = [part[1] for part in parts]
    top = functools.reduce(jnp.maximum, tops)
    scales = [jnp.exp(one - top) for one in tops]
    sums = [
        sum(tile * scale for tile, scale in zip(tiles, scales))
        for tiles in zip(*[part[0] for part in parts])
    ]
    return sums, top, sum(part[2] * scale for part, scale in zip(parts, scales))


def shared_out(sums, top, total, keep_ref, send_refs):
    rows = keep_ref.shape[0]
    packed(
        keep_ref,
        jnp.concatenate([tile[:rows] for tile in sums], axis=1),
        top[:rows],
        total[:rows],
    )
    for index, ref in enumerate(send_refs):
        here = slice((index + 1) * rows, (index + 2) * rows)
        parcel(ref, [tile[here] for tile in sums], top[here], total[here])


def first_combine_kernel(left_ref, right_ref, centre_ref, keep_ref, *send_refs):
    sums, top, total = combined([loaded(left_ref), loaded(right_ref)])
    sums = [
        tile - total * centre_ref[:, pl.ds(index * LANES, LANES)]
        for index, tile in enumerate(sums)
    ]
    shared_out(sums, top, total, keep_ref, send_refs)


def next_combine_kernel(arrived, left_ref, *refs):
    right_refs, keep_ref, send_refs = refs[:arrived], refs[arrived], refs[arrived + 1 :]
    parts = [loaded(left_ref)] + [opened(ref) for ref in right_refs]
    shared_out(*combined(parts), keep_ref, send_refs)


def combine(left, rights, sends, centres=None):
    rows, width = left.shape[0] // (1 + sends), left.shape[1]
    more = () if centres is None else (centres,)
    return pl.pallas_call(
        functools.partial(next_combine_kernel, len(rights))
        if centres is None
        else first_combine_kernel,
        out_shape=(jax.ShapeDtypeStruct((rows, width), F32),)
        + (jax.ShapeDtypeStruct((rows, width), BF16),) * sends,
        in_specs=[VMEM] * (1 + len(rights) + len(more)),
        out_specs=(VMEM,) * (1 + sends),
        compiler_params=pltpu.CompilerParams(vmem_limit_bytes=SMALL),
        name="combine",
    )(left, *rights, *more)


def self_kernel(near_ref, far_ref, *refs):
    visits = (len(refs) - 2) // 2
    visit_refs, centre_ref, out_refs = refs[:visits], refs[visits], refs[visits + 1 :]
    near = near_ref.shape[0]
    rows = jnp.concatenate([near_ref[...]] + [ref[...] for ref in visit_refs], axis=0)
    wide = rows.astype(F32)
    rows_sq = jnp.sum(wide * wide, axis=1, keepdims=True) * HALF
    scaled = rows * BF16(2.0 * HALF)
    columns = jnp.concatenate([near_ref[...], far_ref[...]], axis=0)
    dots = lax.dot_general(scaled, columns, NT, preferred_element_type=F32)
    scores = dots - rows_sq - lane_square_norms(columns)[0:1] * HALF
    row_id = lax.broadcasted_iota(jnp.int32, scores.shape, 0)
    same = (row_id == lax.broadcasted_iota(jnp.int32, scores.shape, 1)) & (row_id < near)
    scores = jnp.where(same, -1e30, scores)
    top = jnp.max(scores, axis=1, keepdims=True)
    weights = jnp.where(same, 0.0, jnp.exp(scores - top))
    total = jnp.sum(weights, axis=1, keepdims=True)
    sums = jnp.dot(weights.astype(BF16), columns, preferred_element_type=F32)
    centre_ref[...] = sums[:near] / total[:near]
    size = out_refs[0].shape[0]
    for first, ref in zip([0] + [near + k * size for k in range(visits)], out_refs):
        here = slice(first, first + size)
        packed(ref, sums[here], top[here], total[here])


def self_terms(near, far, visitors, size):
    width = near.shape[1]
    part = jax.ShapeDtypeStruct((size, width + LANES), F32)
    return pl.pallas_call(
        self_kernel,
        out_shape=(jax.ShapeDtypeStruct(near.shape, F32),) + (part,) * (1 + len(visitors)),
        in_specs=[VMEM] * (2 + len(visitors)),
        out_specs=(VMEM,) * (2 + len(visitors)),
        compiler_params=pltpu.CompilerParams(vmem_limit_bytes=SMALL),
        name="self_terms",
    )(near, far, *visitors)


def final_kernel(arrived, own_ref, left_ref, centre_ref, *refs):
    right_refs, self_refs, out_ref = refs[:arrived], refs[arrived:-1], refs[-1]
    rows = own_ref.shape[0]
    sums, _, total = combined([loaded(left_ref)] + [opened(ref) for ref in right_refs])
    self_sums, _, self_total = combined([loaded(ref) for ref in self_refs])
    scale = 1.0 / total
    self_scale = 1.0 / self_total
    for index, (tile, self_tile) in enumerate(zip(sums, self_sums)):
        lanes = pl.ds(index * LANES, LANES)
        cross_mean = tile * scale + centre_ref[0:rows, lanes]
        out_ref[:, lanes] = own_ref[:, lanes].astype(F32) + STEP_SIZE * (
            cross_mean - self_tile * self_scale
        )


def final(own, left, centres, rights, self_parts):
    return pl.pallas_call(
        functools.partial(final_kernel, len(rights)),
        out_shape=jax.ShapeDtypeStruct(own.shape, F32),
        in_specs=[VMEM] * (3 + len(rights) + len(self_parts)),
        out_specs=VMEM,
        compiler_params=pltpu.CompilerParams(vmem_limit_bytes=SMALL),
        name="final",
    )(own, left, centres, *rights, *self_parts)


def swap(values, mask):
    size = lax.axis_size("ref")
    return lax.ppermute(values, "ref", [(i, i ^ mask) for i in range(size)])


def across(values, shift):
    groups, size = lax.axis_size("grp"), lax.axis_size("ref")
    pairs = [
        (g * size + i, (g + shift) % groups * size + (i ^ 1))
        for g in range(groups)
        for i in range(size)
    ]
    return lax.ppermute(values, ("grp", "ref"), pairs)


def swap_masks(size):
    count = size.bit_length() - 1
    assert size == 1 << count and count >= 4
    low, high = 1 << (count - 2), 1 << (count - 1)
    singles = [1] + [(1 << k) | 1 for k in range(1, count - 2)]
    return singles, [high | low | 1, low, high | 1]


def per_device(particles, samples):
    grp_size = lax.axis_size("grp")
    singles, triple = swap_masks(lax.axis_size("ref"))
    count = samples.shape[0]
    own, staged, *first_part = stage(particles, samples, count * STAGED // 4, 8)
    prepared = [first_part]
    others = [swap(particles, mask) for mask in triple]
    block = join([own] + others, 1, first_part[1:])
    prepared += [
        prepare(staged, part * count // 4, count // 4, [block]) for part in range(STAGED, 4)
    ]
    for mask in reversed(singles[1:]):
        block = join([block, swap(block, mask)], 1 + len(triple), prepared[-1][1:])
    far_block = swap(block, singles[0])
    keep, send = cross_terms(block, far_block, staged, prepared)
    visitors = [across(own, k) for k in range(1, grp_size)]
    centres, *self_parts = self_terms(block, far_block, visitors, own.shape[0])
    returned = [across(part, -k) for k, part in zip(range(1, grp_size), self_parts[1:])]
    keep, *sends = combine(keep, [swap(send, singles[0])], len(triple), centres)
    rights = [swap(part, mask) for part, mask in zip(sends, triple)]
    for mask in singles[1:]:
        keep, send = combine(keep, rights, 1)
        rights = [swap(send, mask)]
    return final(own, keep, centres, rights, [self_parts[0]] + returned)


def solution(mesh):
    in_specs = (P(("grp", "ref"), None), P("ref", None))
    out_specs = P(("grp", "ref"), None)

    return jax.shard_map(
        per_device, mesh=mesh, in_specs=in_specs, out_specs=out_specs, check_vma=False
    )
```

```python
import functools

import jax
import jax.numpy as jnp
from jax import lax
from jax.experimental import pallas as pl
from jax.experimental.pallas import tpu as pltpu
from jax.sharding import PartitionSpec as P


KERNEL_WIDTH = 16
STEP_SIZE = 8.0
LANES = 128
NT = (((1,), (1,)), ((), ()))
VMEM = pl.BlockSpec(memory_space=pltpu.VMEM)
ANY = pl.BlockSpec(memory_space=pl.ANY)
HBM = pl.BlockSpec(memory_space=pltpu.HBM)
SMALL = 2 << 20
STAGED = 2
F32 = jnp.float32
BF16 = jnp.bfloat16
HALF = 1.0 / (2.0 * KERNEL_WIDTH)


def lane_square_norms(values):
    partial = None
    for start in range(0, values.shape[1], LANES):
        wide = values[:, start : start + LANES].astype(F32)
        partial = wide * wide if partial is None else partial + wide * wide
    high = partial.astype(BF16)
    rest = partial - high.astype(F32)
    mid = rest.astype(BF16)
    low = (rest - mid.astype(F32)).astype(BF16)
    ones = jnp.ones((8, LANES), BF16)

    def summed(part):
        return lax.dot_general(ones, part, NT, preferred_element_type=F32)

    return summed(low) + summed(mid) + summed(high)


def turned_block(block, turned_ref, norm_ref, columns):
    turned = jnp.transpose(block)
    turned_ref[:, columns] = turned
    wide = turned.astype(F32)
    norm = jnp.sum(wide * wide, axis=0, keepdims=True) * HALF
    norm_ref[:, columns] = jnp.broadcast_to(norm, (8, norm.shape[1]))


def prepare_kernel(first, samples_ref, *refs):
    turned_ref, norm_ref = refs[-2:]
    count = turned_ref.shape[1]
    tile = min(512, count)
    for start in range(0, count, tile):
        block = samples_ref[pl.ds(first + start, tile), :]
        turned_block(block, turned_ref, norm_ref, pl.ds(start, tile))


def prepare(samples, first, count, after=()):
    width = samples.shape[1]
    return pl.pallas_call(
        functools.partial(prepare_kernel, first),
        out_shape=(
            jax.ShapeDtypeStruct((width, count), samples.dtype),
            jax.ShapeDtypeStruct((8, count), F32),
        ),
        in_specs=[VMEM] + [ANY] * len(after),
        out_specs=(VMEM, VMEM),
        compiler_params=pltpu.CompilerParams(vmem_limit_bytes=SMALL),
        cost_estimate=pl.CostEstimate(
            flops=2 * count * width, bytes_accessed=4 * count * width, transcendentals=0
        ),
        name="prepare",
    )(samples, *after)


def stage_kernel(own_ref, samples_ref, own_out, samples_out, turned_out, norm_out, sems):
    count = samples_ref.shape[0]
    chunks = sems.shape[0] - 1
    size = count // chunks
    own_copy = pltpu.make_async_copy(own_ref, own_out, sems.at[chunks])
    own_copy.start()
    copies = []
    for k in range(chunks):
        rows = pl.ds(k * size, size)
        copies.append(
            pltpu.make_async_copy(samples_ref.at[rows], samples_out.at[rows], sems.at[k])
        )
        copies[-1].start()
    own_copy.wait()
    for k in range(chunks):
        copies[k].wait()
        if k * size < norm_out.shape[1]:
            rows = pl.ds(k * size, size)
            turned_block(samples_out[rows, :], turned_out, norm_out, rows)


def in_hbm(array):
    return pltpu.with_memory_space_constraint(array, pltpu.HBM)


def stage(own, samples, first_count, chunks):
    return pl.pallas_call(
        stage_kernel,
        out_shape=(
            pltpu.VMEM(own.shape, own.dtype),
            pltpu.VMEM(samples.shape, samples.dtype),
            pltpu.VMEM((samples.shape[1], first_count), samples.dtype),
            pltpu.VMEM((8, first_count), F32),
        ),
        in_specs=[HBM, HBM],
        out_specs=(VMEM, VMEM, VMEM, VMEM),
        scratch_shapes=[pltpu.SemaphoreType.DMA((chunks + 1,))],
        compiler_params=pltpu.CompilerParams(vmem_limit_bytes=SMALL),
        name="stage",
    )(in_hbm(own), in_hbm(samples))


def join_kernel(count, runs, *refs):
    blocks = [ref[...] for ref in refs[:count]]
    size = blocks[0].shape[0] // runs
    refs[-1][...] = jnp.concatenate(
        [block[run * size : (run + 1) * size] for run in range(runs) for block in blocks], axis=0
    )


def join(blocks, runs, after=()):
    rows, width = blocks[0].shape
    return pl.pallas_call(
        functools.partial(join_kernel, len(blocks), runs),
        out_shape=jax.ShapeDtypeStruct((len(blocks) * rows, width), blocks[0].dtype),
        in_specs=[VMEM] * len(blocks) + [ANY] * len(after),
        out_specs=VMEM,
        compiler_params=pltpu.CompilerParams(vmem_limit_bytes=SMALL),
        name="join",
    )(*blocks, *after)


def packed(ref, sums, top, total):
    width = sums.shape[1]
    lane_id = lax.broadcasted_iota(jnp.int32, (sums.shape[0], LANES), 1)
    ref[:, 0:width] = sums
    ref[:, width : width + LANES] = jnp.where(lane_id < LANES // 2, top, total)


def regrouped(near, far, picks):
    size = near.shape[0] // len(picks)
    runs = [
        [block[run * size : (run + 1) * size] for run in range(len(picks))] for block in (near, far)
    ]
    return jnp.concatenate(
        [runs[side][run] for side, run in picks] + [runs[1 - side][run] for side, run in picks],
        axis=0,
    )


def cross_kernel(picks, near_ref, far_ref, samples_ref, *refs):
    near_out, far_out = refs[-2:]
    turned_refs, norm_refs = refs[0:-2:2], refs[1:-2:2]
    group = regrouped(near_ref[...], far_ref[...], picks)
    rows, _ = group.shape
    wide = group.astype(F32)
    group_sq = jnp.sum(wide * wide, axis=1, keepdims=True) * HALF
    scaled = group * BF16(2.0 * HALF)
    tiles, start = [], 0
    for first, last in ((0, 1), (1, len(turned_refs))):
        chunks = []
        for turned_ref, norm_ref in zip(turned_refs[first:last], norm_refs[first:last]):
            dots = jnp.dot(scaled, turned_ref[...], preferred_element_type=F32)
            chunks.append(dots - norm_ref[0:1, :])
        scores = jnp.concatenate(chunks, axis=1)
        count = scores.shape[1]
        lanes = [slice(lane, lane + LANES) for lane in range(0, count, LANES)]
        peak = functools.reduce(jnp.maximum, [scores[:, lane] for lane in lanes])
        top = jnp.max(peak, axis=1, keepdims=True)
        weights = jnp.exp(scores - top)
        partial = functools.reduce(jnp.add, [weights[:, lane] for lane in lanes])
        sums = jnp.dot(
            weights.astype(BF16), samples_ref[pl.ds(start, count), :], preferred_element_type=F32
        )
        tiles.append((top, partial, sums))
        start += count
    top = jnp.maximum(tiles[0][0], tiles[1][0])
    scales = [jnp.exp(tile[0] - top) for tile in tiles]
    partial = sum(tile[1] * scale for tile, scale in zip(tiles, scales))
    sums = sum(tile[2] * scale for tile, scale in zip(tiles, scales))
    total = jnp.sum(partial, axis=1, keepdims=True)
    top = top - group_sq
    half = rows // 2
    packed(near_out, sums[:half], top[:half], total[:half])
    packed(far_out, sums[half:], top[half:], total[half:])


def cross_terms(near, far, samples, prepared, picks):
    count, width = samples.shape
    rows = near.shape[0] + far.shape[0]
    part = jax.ShapeDtypeStruct((rows // 2, width + LANES), F32)
    return pl.pallas_call(
        functools.partial(cross_kernel, picks),
        out_shape=(part, part),
        in_specs=[VMEM] * (3 + 2 * len(prepared)),
        out_specs=(VMEM, VMEM),
        compiler_params=pltpu.CompilerParams(vmem_limit_bytes=12 << 20),
        cost_estimate=pl.CostEstimate(
            flops=4 * rows * count * width,
            bytes_accessed=4 * count * width,
            transcendentals=rows * count,
        ),
        name="cross_terms",
    )(near, far, samples, *[array for pair in prepared for array in pair])


def split_stats(stats):
    lane_id = lax.broadcasted_iota(jnp.int32, stats.shape, 1)
    left = lane_id < LANES // 2
    turned = pltpu.roll(stats, LANES // 2, 1)
    return jnp.where(left, stats, turned), jnp.where(left, turned, stats)


def three_parts(values):
    high = values.astype(BF16).astype(F32)
    rest = values - high
    mid = rest.astype(BF16).astype(F32)
    return high, mid, rest - mid


def parcel(ref, sums, top, total):
    lane_id = lax.broadcasted_iota(jnp.int32, top.shape, 1)
    stats = jnp.zeros_like(top)
    for index, part in enumerate(three_parts(top) + three_parts(total)):
        stats = jnp.where(lane_id == index, part, stats)
    for index, tile in enumerate(sums + [stats]):
        ref[:, pl.ds(index * LANES, LANES)] = tile.astype(BF16)


def opened(ref):
    tiles = [
        ref[:, pl.ds(lane, LANES)].astype(F32) for lane in range(0, ref.shape[1], LANES)
    ]
    stats = tiles.pop()
    parts = [jnp.broadcast_to(stats[:, k : k + 1], stats.shape) for k in range(6)]
    return tiles, parts[2] + parts[1] + parts[0], parts[5] + parts[4] + parts[3]


def loaded(ref):
    width = ref.shape[1] - LANES
    top, total = split_stats(ref[:, width : width + LANES])
    return [ref[:, pl.ds(lane, LANES)] for lane in range(0, width, LANES)], top, total


def combined(parts):
    tops = [part[1] for part in parts]
    top = functools.reduce(jnp.maximum, tops)
    scales = [jnp.exp(one - top) for one in tops]
    sums = [
        sum(tile * scale for tile, scale in zip(tiles, scales))
        for tiles in zip(*[part[0] for part in parts])
    ]
    return sums, top, sum(part[2] * scale for part, scale in zip(parts, scales))


def shared_out(sums, top, total, keep_ref, send_refs):
    rows = keep_ref.shape[0]
    packed(
        keep_ref,
        jnp.concatenate([tile[:rows] for tile in sums], axis=1),
        top[:rows],
        total[:rows],
    )
    for index, ref in enumerate(send_refs):
        here = slice((index + 1) * rows, (index + 2) * rows)
        parcel(ref, [tile[here] for tile in sums], top[here], total[here])


def first_combine_kernel(left_ref, right_ref, centre_ref, keep_ref, *send_refs):
    sums, top, total = combined([loaded(left_ref), loaded(right_ref)])
    sums = [
        tile - total * centre_ref[:, pl.ds(index * LANES, LANES)]
        for index, tile in enumerate(sums)
    ]
    shared_out(sums, top, total, keep_ref, send_refs)


def next_combine_kernel(arrived, left_ref, *refs):
    right_refs, keep_ref, send_refs = refs[:arrived], refs[arrived], refs[arrived + 1 :]
    parts = [loaded(left_ref)] + [opened(ref) for ref in right_refs]
    shared_out(*combined(parts), keep_ref, send_refs)


def combine(left, rights, sends, centres=None):
    rows, width = left.shape[0] // (1 + sends), left.shape[1]
    more = () if centres is None else (centres,)
    return pl.pallas_call(
        functools.partial(next_combine_kernel, len(rights))
        if centres is None
        else first_combine_kernel,
        out_shape=(jax.ShapeDtypeStruct((rows, width), F32),)
        + (jax.ShapeDtypeStruct((rows, width), BF16),) * sends,
        in_specs=[VMEM] * (1 + len(rights) + len(more)),
        out_specs=(VMEM,) * (1 + sends),
        compiler_params=pltpu.CompilerParams(vmem_limit_bytes=SMALL),
        name="combine",
    )(left, *rights, *more)


def self_kernel(picks, near_ref, far_ref, *refs):
    visits = (len(refs) - 2) // 2
    visit_refs, centre_ref, out_refs = refs[:visits], refs[visits], refs[visits + 1 :]
    near = near_ref.shape[0]
    columns = regrouped(near_ref[...], far_ref[...], picks)
    rows = jnp.concatenate([columns[:near]] + [ref[...] for ref in visit_refs], axis=0)
    wide = rows.astype(F32)
    rows_sq = jnp.sum(wide * wide, axis=1, keepdims=True) * HALF
    scaled = rows * BF16(2.0 * HALF)
    dots = lax.dot_general(scaled, columns, NT, preferred_element_type=F32)
    scores = dots - rows_sq - lane_square_norms(columns)[0:1] * HALF
    row_id = lax.broadcasted_iota(jnp.int32, scores.shape, 0)
    same = (row_id == lax.broadcasted_iota(jnp.int32, scores.shape, 1)) & (row_id < near)
    scores = jnp.where(same, -1e30, scores)
    top = jnp.max(scores, axis=1, keepdims=True)
    weights = jnp.where(same, 0.0, jnp.exp(scores - top))
    total = jnp.sum(weights, axis=1, keepdims=True)
    sums = jnp.dot(weights.astype(BF16), columns, preferred_element_type=F32)
    centre_ref[...] = sums[:near] / total[:near]
    size = out_refs[0].shape[0]
    for first, ref in zip([0] + [near + k * size for k in range(visits)], out_refs):
        here = slice(first, first + size)
        packed(ref, sums[here], top[here], total[here])


def self_terms(near, far, visitors, size, picks):
    width = near.shape[1]
    part = jax.ShapeDtypeStruct((size, width + LANES), F32)
    return pl.pallas_call(
        functools.partial(self_kernel, picks),
        out_shape=(jax.ShapeDtypeStruct(near.shape, F32),) + (part,) * (1 + len(visitors)),
        in_specs=[VMEM] * (2 + len(visitors)),
        out_specs=(VMEM,) * (2 + len(visitors)),
        compiler_params=pltpu.CompilerParams(vmem_limit_bytes=SMALL),
        name="self_terms",
    )(near, far, *visitors)


def final_kernel(arrived, own_ref, left_ref, centre_ref, *refs):
    right_refs, self_refs, out_ref = refs[:arrived], refs[arrived:-1], refs[-1]
    rows = own_ref.shape[0]
    sums, _, total = combined([loaded(left_ref)] + [opened(ref) for ref in right_refs])
    self_sums, _, self_total = combined([loaded(ref) for ref in self_refs])
    scale = 1.0 / total
    self_scale = 1.0 / self_total
    for index, (tile, self_tile) in enumerate(zip(sums, self_sums)):
        lanes = pl.ds(index * LANES, LANES)
        cross_mean = tile * scale + centre_ref[0:rows, lanes]
        out_ref[:, lanes] = own_ref[:, lanes].astype(F32) + STEP_SIZE * (
            cross_mean - self_tile * self_scale
        )


def final(own, left, centres, rights, self_parts):
    return pl.pallas_call(
        functools.partial(final_kernel, len(rights)),
        out_shape=jax.ShapeDtypeStruct(own.shape, F32),
        in_specs=[VMEM] * (3 + len(rights) + len(self_parts)),
        out_specs=VMEM,
        compiler_params=pltpu.CompilerParams(vmem_limit_bytes=SMALL),
        name="final",
    )(own, left, centres, *rights, *self_parts)


def swap(values, mask):
    size = lax.axis_size("ref")
    return lax.ppermute(values, "ref", [(i, i ^ mask) for i in range(size)])


def across(values, shift):
    groups, size = lax.axis_size("grp"), lax.axis_size("ref")
    pairs = [
        (g * size + i, (g + shift) % groups * size + (i ^ 1))
        for g in range(groups)
        for i in range(size)
    ]
    return lax.ppermute(values, ("grp", "ref"), pairs)


def swap_masks(size):
    count = size.bit_length() - 1
    assert size == 1 << count and count >= 4
    low, high = 1 << (count - 2), 1 << (count - 1)
    singles = [1] + [(1 << k) | 1 for k in range(1, count - 2)]
    return singles, [low | 1, high | low, high | 1], [high | low | 1, low, high | 1]


def per_device(particles, samples):
    grp_size = lax.axis_size("grp")
    singles, gathers, triple = swap_masks(lax.axis_size("ref"))
    count = samples.shape[0]
    own, staged, *first_part = stage(particles, samples, count * STAGED // 4, 8)
    prepared = [first_part]
    others = [swap(particles, mask) for mask in gathers]
    block = join([own] + others, 1, first_part[1:])
    prepared += [
        prepare(staged, part * count // 4, count // 4, [block]) for part in range(STAGED, 4)
    ]
    for mask in reversed(singles[1:]):
        block = join([block, swap(block, mask)], 1 + len(triple), prepared[-1][1:])
    far_block = swap(block, singles[0])
    arrived = [0] + gathers
    picks = [
        (0, arrived.index(mask)) if mask in arrived else (1, arrived.index(mask ^ 1))
        for mask in [0] + triple
    ]
    keep, send = cross_terms(block, far_block, staged, prepared, picks)
    visitors = [across(own, k) for k in range(1, grp_size)]
    centres, *self_parts = self_terms(block, far_block, visitors, own.shape[0], picks)
    returned = [across(part, -k) for k, part in zip(range(1, grp_size), self_parts[1:])]
    keep, *sends = combine(keep, [swap(send, singles[0])], len(triple), centres)
    rights = [swap(part, mask) for part, mask in zip(sends, triple)]
    for mask in singles[1:]:
        keep, send = combine(keep, rights, 1)
        rights = [swap(send, mask)]
    return final(own, keep, centres, rights, [self_parts[0]] + returned)


def solution(mesh):
    in_specs = (P(("grp", "ref"), None), P("ref", None))
    out_specs = P(("grp", "ref"), None)

    return jax.shard_map(
        per_device, mesh=mesh, in_specs=in_specs, out_specs=out_specs, check_vma=False
    )
```

```python
import functools

import jax
import jax.numpy as jnp
from jax import lax
from jax.experimental import pallas as pl
from jax.experimental.pallas import tpu as pltpu
from jax.sharding import PartitionSpec as P


KERNEL_WIDTH = 16
STEP_SIZE = 8.0
LANES = 128
NT = (((1,), (1,)), ((), ()))
VMEM = pl.BlockSpec(memory_space=pltpu.VMEM)
ANY = pl.BlockSpec(memory_space=pl.ANY)
HBM = pl.BlockSpec(memory_space=pltpu.HBM)
SMALL = 2 << 20
STAGED = 3
F32 = jnp.float32
BF16 = jnp.bfloat16
HALF = 1.0 / (2.0 * KERNEL_WIDTH)


def lane_square_norms(values):
    partial = None
    for start in range(0, values.shape[1], LANES):
        wide = values[:, start : start + LANES].astype(F32)
        partial = wide * wide if partial is None else partial + wide * wide
    high = partial.astype(BF16)
    rest = partial - high.astype(F32)
    mid = rest.astype(BF16)
    low = (rest - mid.astype(F32)).astype(BF16)
    ones = jnp.ones((8, LANES), BF16)

    def summed(part):
        return lax.dot_general(ones, part, NT, preferred_element_type=F32)

    return summed(low) + summed(mid) + summed(high)


def turned_block(block, turned_ref, norm_ref, columns):
    turned = jnp.transpose(block)
    turned_ref[:, columns] = turned
    wide = turned.astype(F32)
    norm = jnp.sum(wide * wide, axis=0, keepdims=True) * HALF
    norm_ref[:, columns] = jnp.broadcast_to(norm, (8, norm.shape[1]))


def prepare_kernel(first, samples_ref, *refs):
    turned_ref, norm_ref = refs[-2:]
    count = turned_ref.shape[1]
    tile = min(512, count)
    for start in range(0, count, tile):
        block = samples_ref[pl.ds(first + start, tile), :]
        turned_block(block, turned_ref, norm_ref, pl.ds(start, tile))


def prepare(samples, first, count, after=()):
    width = samples.shape[1]
    return pl.pallas_call(
        functools.partial(prepare_kernel, first),
        out_shape=(
            jax.ShapeDtypeStruct((width, count), samples.dtype),
            jax.ShapeDtypeStruct((8, count), F32),
        ),
        in_specs=[VMEM] + [ANY] * len(after),
        out_specs=(VMEM, VMEM),
        compiler_params=pltpu.CompilerParams(vmem_limit_bytes=SMALL),
        cost_estimate=pl.CostEstimate(
            flops=2 * count * width, bytes_accessed=4 * count * width, transcendentals=0
        ),
        name="prepare",
    )(samples, *after)


def stage_kernel(own_ref, samples_ref, own_out, samples_out, turned_out, norm_out, sems):
    count = samples_ref.shape[0]
    chunks = sems.shape[0] - 1
    size = count // chunks
    own_copy = pltpu.make_async_copy(own_ref, own_out, sems.at[chunks])
    own_copy.start()
    copies = []
    for k in range(chunks):
        rows = pl.ds(k * size, size)
        copies.append(
            pltpu.make_async_copy(samples_ref.at[rows], samples_out.at[rows], sems.at[k])
        )
        copies[-1].start()
    own_copy.wait()
    for k in range(chunks):
        copies[k].wait()
        if k * size < norm_out.shape[1]:
            rows = pl.ds(k * size, size)
            turned_block(samples_out[rows, :], turned_out, norm_out, rows)


def in_hbm(array):
    return pltpu.with_memory_space_constraint(array, pltpu.HBM)


def stage(own, samples, first_count, chunks):
    return pl.pallas_call(
        stage_kernel,
        out_shape=(
            pltpu.VMEM(own.shape, own.dtype),
            pltpu.VMEM(samples.shape, samples.dtype),
            pltpu.VMEM((samples.shape[1], first_count), samples.dtype),
            pltpu.VMEM((8, first_count), F32),
        ),
        in_specs=[HBM, HBM],
        out_specs=(VMEM, VMEM, VMEM, VMEM),
        scratch_shapes=[pltpu.SemaphoreType.DMA((chunks + 1,))],
        compiler_params=pltpu.CompilerParams(vmem_limit_bytes=SMALL),
        name="stage",
    )(in_hbm(own), in_hbm(samples))


def join_kernel(count, runs, *refs):
    blocks = [ref[...] for ref in refs[:count]]
    size = blocks[0].shape[0] // runs
    refs[-1][...] = jnp.concatenate(
        [block[run * size : (run + 1) * size] for run in range(runs) for block in blocks], axis=0
    )


def join(blocks, runs, after=()):
    rows, width = blocks[0].shape
    return pl.pallas_call(
        functools.partial(join_kernel, len(blocks), runs),
        out_shape=jax.ShapeDtypeStruct((len(blocks) * rows, width), blocks[0].dtype),
        in_specs=[VMEM] * len(blocks) + [ANY] * len(after),
        out_specs=VMEM,
        compiler_params=pltpu.CompilerParams(vmem_limit_bytes=SMALL),
        name="join",
    )(*blocks, *after)


def packed(ref, sums, top, total):
    width = sums.shape[1]
    lane_id = lax.broadcasted_iota(jnp.int32, (sums.shape[0], LANES), 1)
    ref[:, 0:width] = sums
    ref[:, width : width + LANES] = jnp.where(lane_id < LANES // 2, top, total)


def regrouped(near, far, picks):
    size = near.shape[0] // len(picks)
    runs = [
        [block[run * size : (run + 1) * size] for run in range(len(picks))] for block in (near, far)
    ]
    return jnp.concatenate(
        [runs[side][run] for side, run in picks] + [runs[1 - side][run] for side, run in picks],
        axis=0,
    )


def cross_kernel(picks, near_ref, far_ref, samples_ref, *refs):
    near_out, far_out = refs[-2:]
    turned_refs, norm_refs = refs[0:-2:2], refs[1:-2:2]
    group = regrouped(near_ref[...], far_ref[...], picks)
    rows, _ = group.shape
    wide = group.astype(F32)
    group_sq = jnp.sum(wide * wide, axis=1, keepdims=True) * HALF
    scaled = group * BF16(2.0 * HALF)
    tiles, start = [], 0
    for first, last in ((0, 1), (1, len(turned_refs))):
        chunks = []
        for turned_ref, norm_ref in zip(turned_refs[first:last], norm_refs[first:last]):
            dots = jnp.dot(scaled, turned_ref[...], preferred_element_type=F32)
            chunks.append(dots - norm_ref[0:1, :])
        scores = jnp.concatenate(chunks, axis=1)
        count = scores.shape[1]
        lanes = [slice(lane, lane + LANES) for lane in range(0, count, LANES)]
        peak = functools.reduce(jnp.maximum, [scores[:, lane] for lane in lanes])
        top = jnp.max(peak, axis=1, keepdims=True)
        weights = jnp.exp(scores - top)
        partial = functools.reduce(jnp.add, [weights[:, lane] for lane in lanes])
        sums = jnp.dot(
            weights.astype(BF16), samples_ref[pl.ds(start, count), :], preferred_element_type=F32
        )
        tiles.append((top, partial, sums))
        start += count
    top = jnp.maximum(tiles[0][0], tiles[1][0])
    scales = [jnp.exp(tile[0] - top) for tile in tiles]
    partial = sum(tile[1] * scale for tile, scale in zip(tiles, scales))
    sums = sum(tile[2] * scale for tile, scale in zip(tiles, scales))
    total = jnp.sum(partial, axis=1, keepdims=True)
    top = top - group_sq
    half = rows // 2
    packed(near_out, sums[:half], top[:half], total[:half])
    packed(far_out, sums[half:], top[half:], total[half:])


def cross_terms(near, far, samples, prepared, picks):
    count, width = samples.shape
    rows = near.shape[0] + far.shape[0]
    part = jax.ShapeDtypeStruct((rows // 2, width + LANES), F32)
    return pl.pallas_call(
        functools.partial(cross_kernel, picks),
        out_shape=(part, part),
        in_specs=[VMEM] * (3 + 2 * len(prepared)),
        out_specs=(VMEM, VMEM),
        compiler_params=pltpu.CompilerParams(vmem_limit_bytes=12 << 20),
        cost_estimate=pl.CostEstimate(
            flops=4 * rows * count * width,
            bytes_accessed=4 * count * width,
            transcendentals=rows * count,
        ),
        name="cross_terms",
    )(near, far, samples, *[array for pair in prepared for array in pair])


def split_stats(stats):
    lane_id = lax.broadcasted_iota(jnp.int32, stats.shape, 1)
    left = lane_id < LANES // 2
    turned = pltpu.roll(stats, LANES // 2, 1)
    return jnp.where(left, stats, turned), jnp.where(left, turned, stats)


def three_parts(values):
    high = values.astype(BF16).astype(F32)
    rest = values - high
    mid = rest.astype(BF16).astype(F32)
    return high, mid, rest - mid


def parcel(ref, sums, top, total):
    lane_id = lax.broadcasted_iota(jnp.int32, top.shape, 1)
    stats = jnp.zeros_like(top)
    for index, part in enumerate(three_parts(top) + three_parts(total)):
        stats = jnp.where(lane_id == index, part, stats)
    for index, tile in enumerate(sums + [stats]):
        ref[:, pl.ds(index * LANES, LANES)] = tile.astype(BF16)


def opened(ref):
    tiles = [
        ref[:, pl.ds(lane, LANES)].astype(F32) for lane in range(0, ref.shape[1], LANES)
    ]
    stats = tiles.pop()
    parts = [jnp.broadcast_to(stats[:, k : k + 1], stats.shape) for k in range(6)]
    return tiles, parts[2] + parts[1] + parts[0], parts[5] + parts[4] + parts[3]


def loaded(ref):
    width = ref.shape[1] - LANES
    top, total = split_stats(ref[:, width : width + LANES])
    return [ref[:, pl.ds(lane, LANES)] for lane in range(0, width, LANES)], top, total


def combined(parts):
    tops = [part[1] for part in parts]
    top = functools.reduce(jnp.maximum, tops)
    scales = [jnp.exp(one - top) for one in tops]
    sums = [
        sum(tile * scale for tile, scale in zip(tiles, scales))
        for tiles in zip(*[part[0] for part in parts])
    ]
    return sums, top, sum(part[2] * scale for part, scale in zip(parts, scales))


def shared_out(sums, top, total, keep_ref, send_refs):
    rows = keep_ref.shape[0]
    packed(
        keep_ref,
        jnp.concatenate([tile[:rows] for tile in sums], axis=1),
        top[:rows],
        total[:rows],
    )
    for index, ref in enumerate(send_refs):
        here = slice((index + 1) * rows, (index + 2) * rows)
        parcel(ref, [tile[here] for tile in sums], top[here], total[here])


def first_combine_kernel(left_ref, right_ref, centre_ref, keep_ref, *send_refs):
    sums, top, total = combined([loaded(left_ref), loaded(right_ref)])
    sums = [
        tile - total * centre_ref[:, pl.ds(index * LANES, LANES)]
        for index, tile in enumerate(sums)
    ]
    shared_out(sums, top, total, keep_ref, send_refs)


def next_combine_kernel(arrived, left_ref, *refs):
    right_refs, keep_ref, send_refs = refs[:arrived], refs[arrived], refs[arrived + 1 :]
    parts = [loaded(left_ref)] + [opened(ref) for ref in right_refs]
    shared_out(*combined(parts), keep_ref, send_refs)


def combine(left, rights, sends, centres=None):
    rows, width = left.shape[0] // (1 + sends), left.shape[1]
    more = () if centres is None else (centres,)
    return pl.pallas_call(
        functools.partial(next_combine_kernel, len(rights))
        if centres is None
        else first_combine_kernel,
        out_shape=(jax.ShapeDtypeStruct((rows, width), F32),)
        + (jax.ShapeDtypeStruct((rows, width), BF16),) * sends,
        in_specs=[VMEM] * (1 + len(rights) + len(more)),
        out_specs=(VMEM,) * (1 + sends),
        compiler_params=pltpu.CompilerParams(vmem_limit_bytes=SMALL),
        name="combine",
    )(left, *rights, *more)


def self_kernel(picks, near_ref, far_ref, *refs):
    visits = (len(refs) - 2) // 2
    visit_refs, centre_ref, out_refs = refs[:visits], refs[visits], refs[visits + 1 :]
    near = near_ref.shape[0]
    columns = regrouped(near_ref[...], far_ref[...], picks)
    rows = jnp.concatenate([columns[:near]] + [ref[...] for ref in visit_refs], axis=0)
    wide = rows.astype(F32)
    rows_sq = jnp.sum(wide * wide, axis=1, keepdims=True) * HALF
    scaled = rows * BF16(2.0 * HALF)
    dots = lax.dot_general(scaled, columns, NT, preferred_element_type=F32)
    scores = dots - rows_sq - lane_square_norms(columns)[0:1] * HALF
    row_id = lax.broadcasted_iota(jnp.int32, scores.shape, 0)
    same = (row_id == lax.broadcasted_iota(jnp.int32, scores.shape, 1)) & (row_id < near)
    scores = jnp.where(same, -1e30, scores)
    top = jnp.max(scores, axis=1, keepdims=True)
    weights = jnp.where(same, 0.0, jnp.exp(scores - top))
    total = jnp.sum(weights, axis=1, keepdims=True)
    sums = jnp.dot(weights.astype(BF16), columns, preferred_element_type=F32)
    centre_ref[...] = sums[:near] / total[:near]
    size = out_refs[0].shape[0]
    for first, ref in zip([0] + [near + k * size for k in range(visits)], out_refs):
        here = slice(first, first + size)
        packed(ref, sums[here], top[here], total[here])


def self_terms(near, far, visitors, size, picks):
    width = near.shape[1]
    part = jax.ShapeDtypeStruct((size, width + LANES), F32)
    return pl.pallas_call(
        functools.partial(self_kernel, picks),
        out_shape=(jax.ShapeDtypeStruct(near.shape, F32),) + (part,) * (1 + len(visitors)),
        in_specs=[VMEM] * (2 + len(visitors)),
        out_specs=(VMEM,) * (2 + len(visitors)),
        compiler_params=pltpu.CompilerParams(vmem_limit_bytes=SMALL),
        name="self_terms",
    )(near, far, *visitors)


def final_kernel(arrived, own_ref, left_ref, centre_ref, *refs):
    right_refs, self_refs, out_ref = refs[:arrived], refs[arrived:-1], refs[-1]
    rows = own_ref.shape[0]
    sums, _, total = combined([loaded(left_ref)] + [opened(ref) for ref in right_refs])
    self_sums, _, self_total = combined([loaded(ref) for ref in self_refs])
    scale = 1.0 / total
    self_scale = 1.0 / self_total
    for index, (tile, self_tile) in enumerate(zip(sums, self_sums)):
        lanes = pl.ds(index * LANES, LANES)
        cross_mean = tile * scale + centre_ref[0:rows, lanes]
        out_ref[:, lanes] = own_ref[:, lanes].astype(F32) + STEP_SIZE * (
            cross_mean - self_tile * self_scale
        )


def final(own, left, centres, rights, self_parts):
    return pl.pallas_call(
        functools.partial(final_kernel, len(rights)),
        out_shape=jax.ShapeDtypeStruct(own.shape, F32),
        in_specs=[VMEM] * (3 + len(rights) + len(self_parts)),
        out_specs=VMEM,
        compiler_params=pltpu.CompilerParams(vmem_limit_bytes=SMALL),
        name="final",
    )(own, left, centres, *rights, *self_parts)


def swap(values, mask):
    size = lax.axis_size("ref")
    return lax.ppermute(values, "ref", [(i, i ^ mask) for i in range(size)])


def across(values, shift):
    groups, size = lax.axis_size("grp"), lax.axis_size("ref")
    pairs = [
        (g * size + i, (g + shift) % groups * size + (i ^ 1))
        for g in range(groups)
        for i in range(size)
    ]
    return lax.ppermute(values, ("grp", "ref"), pairs)


def swap_masks(size):
    count = size.bit_length() - 1
    assert size == 1 << count and count >= 4
    low, high = 1 << (count - 2), 1 << (count - 1)
    singles = [1] + [(1 << k) | 1 for k in range(1, count - 2)]
    return singles, [low | 1, high | low, high | 1], [high | low | 1, low, high | 1]


def per_device(particles, samples):
    grp_size = lax.axis_size("grp")
    singles, gathers, triple = swap_masks(lax.axis_size("ref"))
    count = samples.shape[0]
    own, staged, *first_part = stage(particles, samples, count * STAGED // 4, 4)
    prepared = [first_part]
    others = [swap(particles, mask) for mask in gathers]
    block = join([own] + others, 1, first_part[1:])
    for mask in reversed(singles[1:]):
        block = join([block, swap(block, mask)], 1 + len(triple))
    prepared += [
        prepare(staged, part * count // 4, count // 4, [block]) for part in range(STAGED, 4)
    ]
    far_block = swap(block, singles[0])
    arrived = [0] + gathers
    picks = [
        (0, arrived.index(mask)) if mask in arrived else (1, arrived.index(mask ^ 1))
        for mask in [0] + triple
    ]
    keep, send = cross_terms(block, far_block, staged, prepared, picks)
    visitors = [across(own, k) for k in range(1, grp_size)]
    centres, *self_parts = self_terms(block, far_block, visitors, own.shape[0], picks)
    returned = [across(part, -k) for k, part in zip(range(1, grp_size), self_parts[1:])]
    keep, *sends = combine(keep, [swap(send, singles[0])], len(triple), centres)
    rights = [swap(part, mask) for part, mask in zip(sends, triple)]
    for mask in singles[1:]:
        keep, send = combine(keep, rights, 1)
        rights = [swap(send, mask)]
    return final(own, keep, centres, rights, [self_parts[0]] + returned)


def solution(mesh):
    in_specs = (P(("grp", "ref"), None), P("ref", None))
    out_specs = P(("grp", "ref"), None)

    return jax.shard_map(
        per_device, mesh=mesh, in_specs=in_specs, out_specs=out_specs, check_vma=False
    )
```
